32 devices in a mesh: shard: 4 (over y, core), ctx: 2 (over x), tp: 4 (over z).
Axes of the slice: x: 2, y: 2, z: 4, core: 2. Of those that a mesh axis runs over, the one named last changes fastest.
Arguments:
- block_input: bfloat16 [4, 576, 1024], P('shard', 'ctx'), may hold values from -6 to 6
- seg_ids: int32 [4, 576], P('shard'), may hold values from 0 to 1, never falling along the last dimension, each value on 1 to 384 neighbouring positions
- norm1_gain: bfloat16 [1024], P(('shard', 'ctx')), may hold values from 0.5 to 1.5
- zx_weight: bfloat16 [2, 1024, 1536], P(None, ('shard', 'ctx'), 'tp'), may hold values from -0.1875 to 0.1875
- dt_weight: bfloat16 [1024, 24], P(('shard', 'ctx'), 'tp'), may hold values from -0.1875 to 0.1875
- bc_weight: bfloat16 [1024, 256], P(('shard', 'ctx')), may hold values from -0.1875 to 0.1875
- conv_x_weight: float32 [4, 1536], P(None, 'tp'), may hold values from -3 to 3
- conv_x_bias: float32 [1536], P('tp'), may hold values from -3 to 3
- conv_bc_weight: bfloat16 [4, 256], P(None, ('shard', 'ctx')), may hold values from -3 to 3
- conv_bc_bias: bfloat16 [256], P(('shard', 'ctx')), may hold values from -3 to 3
- dt_bias: float32 [24], P('tp'), may hold values from -8 to -3
- a_log: float32 [24], P('tp'), may hold values from -2 to 2.77
- d_skip: float32 [24], P('tp'), may hold values from 0.5 to 1.5
- gnorm_gain: float32 [1536], P('tp'), may hold values from 0.5 to 1.5
- out_weight: bfloat16 [1536, 1024], P('tp', ('shard', 'ctx')), may hold values from -0.15625 to 0.15625
- q_weight: bfloat16 [1024, 512], P(('shard', 'ctx'), 'tp'), may hold values from -0.1875 to 0.1875
- kv_weight: bfloat16 [1024, 256], P(('shard', 'ctx')), may hold values from -0.1875 to 0.1875
- o_weight: bfloat16 [512, 1024], P('tp', ('shard', 'ctx')), may hold values from -1 to 1
- norm2_gain: bfloat16 [1024], P(('shard', 'ctx')), may hold values from 0.5 to 1.5
- gu_weight: bfloat16 [2, 1024, 2048], P(None, ('shard', 'ctx'), 'tp'), may hold values from -0.1875 to 0.1875
- down_weight: bfloat16 [2048, 1024], P('tp', ('shard', 'ctx')), may hold values from -0.125 to 0.125
- d_out: bfloat16 [4, 576, 1024], P('shard', 'ctx'), may hold values from -6 to 6
Outputs:
- block_out: bfloat16 [4, 576, 1024], P('shard', 'ctx')
- input_grad: float32 [4, 576, 1024], P('shard', 'ctx')
- grad_norm1_gain: float32 [1024], P(('shard', 'ctx'))
- grad_zx_weight: float32 [2, 1024, 1536], P(None, ('shard', 'ctx'), 'tp')
- grad_dt_weight: float32 [1024, 24], P(('shard', 'ctx'), 'tp')
- grad_bc_weight: float32 [1024, 256], P(('shard', 'ctx'))
- grad_conv_x_weight: float32 [4, 1536], P(None, 'tp')
- grad_conv_x_bias: float32 [1536], P('tp')
- grad_conv_bc_weight: float32 [4, 256], P(None, ('shard', 'ctx'))
- grad_conv_bc_bias: float32 [256], P(('shard', 'ctx'))
- grad_dt_bias: float32 [24], P('tp')
- grad_a_log: float32 [24], P('tp')
- grad_d_skip: float32 [24], P('tp')
- grad_gnorm_gain: float32 [1536], P('tp')
- grad_out_weight: float32 [1536, 1024], P('tp', ('shard', 'ctx'))
- grad_q_weight: float32 [1024, 512], P(('shard', 'ctx'), 'tp')
- grad_kv_weight: float32 [1024, 256], P(('shard', 'ctx'))
- grad_o_weight: float32 [512, 1024], P('tp', ('shard', 'ctx'))
- grad_norm2_gain: float32 [1024], P(('shard', 'ctx'))
- grad_gu_weight: float32 [2, 1024, 2048], P(None, ('shard', 'ctx'), 'tp')
- grad_down_weight: float32 [2048, 1024], P('tp', ('shard', 'ctx'))
The draws below stay inside these ranges and needn't reach their ends.
Inputs may be any that keep to these rules, and one draw needn't show every extreme that they name: `seg_ids`: segment numbers never fall along a sequence; every sequence holds two documents, each on 192 to 384 neighbouring positions.
All inputs are finite; a program needn't handle non-finite values.
Results may differ from the reference program's by a relative error of at most 0.014.
The reference program's roundings to bfloat16 on the way count: a program that leaves them out, or rounds other values in their place, can miss the bound.
Values may be sent and summed in bfloat16 or wider, within the bound.
No kernel may reach another device: no remote copies, remote signals or barrier semaphores. Data moves between devices by JAX's collectives and lax.ppermute only.
A program may use at most 128 MiB of HBM per device.

```python
import math
import jax
import jax.numpy as jnp
import numpy as np
from jax import lax

D = 1024
HEADS = 24
HDIM = 64
DI = 1536
NST = 128
KCONV = 4
QH = 8
KVH = 2
ADIM = 64
FF = 2048
LEN = 576
SEQS = 4


def block_levels(rng, extent, cuts, smallest, largest):
    def one(position, blocks):
        heights = jax.random.uniform(jax.random.fold_in(jax.random.fold_in(rng, 6), position), (blocks,), jnp.float32, smallest / len(cuts), largest / len(cuts))
        return jnp.repeat(jnp.exp(heights), extent[position] // blocks).reshape((-1,) + (1,) * (len(extent) - position - 1))

    level = one(*cuts[0])
    for cut in cuts[1:]:
        level = level * one(*cut)
    return level


def profile(amount, total, most, slope):
    weights = [(1 << 20) // math.isqrt(rank ** slope) + 1 for rank in range(2, amount + 1)]
    surplus, holding = total - most - (amount - 1), [1] * (amount - 1)
    while surplus > 0:
        movable = [i for i in range(amount - 1) if holding[i] < most]
        pool, remaining = sum([weights[i] for i in movable]), surplus
        for i in movable:
            addition = min(most - holding[i], max(1, remaining * weights[i] // pool), surplus)
            holding[i] = holding[i] + addition
            surplus = surplus - addition
    return np.array([most] + holding)


def uneven(rng, amount, total, most, skew):
    if amount == 2:
        one = jax.random.randint(rng, (), max(1, total - most), min(most, total - 1) + 1)
        return jnp.stack([one, total - one])
    tallies = jnp.asarray(profile(amount, total, most, skew), jnp.int32)
    twos = (amount - 1) // 2
    giver, sink = tallies[1:1 + 2 * twos:2], tallies[2:2 + 2 * twos:2]
    margin = jnp.minimum(giver - 1, most - sink)
    shifted = jax.random.randint(jax.random.fold_in(rng, 1), (twos,), 0, 1 << 20) % (margin + 1)
    tallies = tallies.at[1:1 + 2 * twos:2].set(giver - shifted).at[2:2 + 2 * twos:2].set(sink + shifted)
    return tallies[jax.random.permutation(jax.random.fold_in(rng, 2), amount)]


def normal_values(stream_key, dims, scale, most, pieces=(), held_as=jnp.bfloat16):
    drawn = jax.random.normal(stream_key, dims, jnp.float32) * scale
    if len(pieces) > 0:
        drawn = block_levels(stream_key, dims, pieces, -0.22, 0.18) * drawn
    return jnp.clip(drawn, min=-most, max=most).astype(held_as)


def setup_inputs(seed: int = 0) -> dict:
    splits = jax.random.split(jax.random.key(seed), 23)
    return {
        "block_input": normal_values(splits[0], (SEQS, LEN, D), 1.0, 6.0, ((0, 4), (1, 2))),
        "seg_ids": jax.vmap(lambda own: jnp.searchsorted(jnp.cumsum(uneven(own, 2, LEN, LEN * 2 // 3, 0)), jnp.arange(LEN), side="right"))(jax.random.split(splits[1], SEQS)).reshape((SEQS, LEN)).astype(jnp.int32),
        "norm1_gain": jnp.clip(1.0 + 0.1 * jax.random.normal(splits[2], (D,), jnp.float32), 0.5, 1.5).astype(jnp.bfloat16),
        "zx_weight": normal_values(splits[3], (2, D, DI), D ** -0.5, 0.1875, ((1, 8), (2, 4))),
        "dt_weight": normal_values(splits[4], (D, HEADS), D ** -0.5, 0.1875, ((0, 8), (1, 4))),
        "bc_weight": normal_values(splits[5], (D, 2 * NST), D ** -0.5, 0.1875, ((0, 8),)),
        "conv_x_weight": normal_values(splits[6], (KCONV, DI), KCONV ** -0.5, 3.0, ((1, 4),), jnp.float32),
        "conv_x_bias": normal_values(splits[7], (DI,), 0.5, 3.0, ((0, 4),), jnp.float32),
        "conv_bc_weight": normal_values(splits[8], (KCONV, 2 * NST), KCONV ** -0.5, 3.0, ((1, 8),)),
        "conv_bc_bias": normal_values(splits[9], (2 * NST,), 0.5, 3.0, ((0, 8),)),
        "dt_bias": jnp.clip(-8.0 + 5.0 * jax.random.uniform(splits[10], (HEADS,), jnp.float32) ** block_levels(splits[10], (HEADS,), ((0, 4),), -0.2, 0.2), -8.0, -3.0),
        "a_log": jnp.clip(-2.0 + 4.77 * jax.random.uniform(splits[11], (HEADS,), jnp.float32) ** block_levels(splits[11], (HEADS,), ((0, 4),), -0.2, 0.2), -2.0, 2.77),
        "d_skip": jnp.clip(0.5 + 1.0 * jax.random.uniform(splits[12], (HEADS,), jnp.float32) ** block_levels(splits[12], (HEADS,), ((0, 4),), -0.2, 0.2), 0.5, 1.5),
        "gnorm_gain": jnp.clip(1.0 + 0.1 * jax.random.normal(splits[13], (DI,), jnp.float32), 0.5, 1.5),
        "out_weight": normal_values(splits[14], (DI, D), DI ** -0.5, 0.15625, ((0, 4), (1, 8))),
        "q_weight": normal_values(splits[15], (D, QH * ADIM), D ** -0.5, 0.1875, ((0, 8), (1, 4))),
        "kv_weight": normal_values(splits[16], (D, 2 * KVH * ADIM), D ** -0.5, 0.1875, ((0, 8),)),
        "o_weight": normal_values(splits[17], (QH * ADIM, D), (QH * ADIM // 16) ** -0.5, 1.0, ((0, 4), (1, 8))),
        "norm2_gain": jnp.clip(1.0 + 0.1 * jax.random.normal(splits[18], (D,), jnp.float32), 0.5, 1.5).astype(jnp.bfloat16),
        "gu_weight": normal_values(splits[19], (2, D, FF), D ** -0.5, 0.1875, ((1, 8), (2, 4))),
        "down_weight": normal_values(splits[20], (FF, D), FF ** -0.5, 0.125, ((0, 4), (1, 8))),
        "d_out": normal_values(splits[21], (SEQS, LEN, D), 1.0, 6.0, ((0, 4), (1, 2))),
    }


eps_norm = 1e-05
rope_base = 100000000000.0
highest = lax.Precision.HIGHEST

def rms_factor(values):
    return lax.rsqrt(lax.optimization_barrier(jnp.sum(values * values, axis=-1, keepdims=True)) / values.shape[-1] + eps_norm)

def rms_back(grad_normed, normed, factor):
    return factor * (grad_normed - normed * (lax.optimization_barrier(jnp.sum(grad_normed * normed, axis=-1, keepdims=True)) / normed.shape[-1]))

def inner_rows(left_op, right_op):
    return lax.dot_general(left_op, right_op, (((0,), (0,)), ((), ())), preferred_element_type=jnp.float32)

def inner_cols(left_op, right_op):
    return lax.dot_general(left_op, right_op, (((1,), (1,)), ((), ())), preferred_element_type=jnp.float32)

def rope_tables(positions, width):
    half_width = width // 2
    inverse = jnp.power(rope_base, -(jnp.arange(half_width).astype(jnp.float32) * 2.0 / width))
    angles = positions[:, None] * inverse[None, :]
    return (jnp.cos(angles), jnp.sin(angles))

def rotate(values, cos_table, sin_table):
    half_width = values.shape[-1] // 2
    first_half = values[..., :half_width]
    second = values[..., half_width:]
    cosine = cos_table[:, None, :]
    sine_part = sin_table[:, None, :]
    return jnp.concatenate([first_half * cosine - second * sine_part, second * cosine + first_half * sine_part], axis=-1)

def mamba_section(pre_ext, dt_raw, conv_weight, conv_bias, bias_dt, log_rate, conv_keep, inner_width):
    tap_count = conv_weight.shape[0]
    length = pre_ext.shape[0] - tap_count + 1
    conv_sum = jnp.zeros((length, pre_ext.shape[1]), jnp.float32) + conv_bias[None, :]
    for offset in range(tap_count):
        conv_sum = conv_sum + conv_weight[offset][None, :] * pre_ext[offset:offset + length] * conv_keep[offset][:, None]
    activated = jax.nn.silu(conv_sum)
    heads_here = dt_raw.shape[1]
    state_width = (activated.shape[1] - inner_width) // 2
    inputs = activated[:, :inner_width].reshape(length, heads_here, inner_width // heads_here)
    input_map = activated[:, inner_width:inner_width + state_width]
    output_map = activated[:, inner_width + state_width:]
    delta_time = jax.nn.softplus(dt_raw + bias_dt[None, :])
    cum_decay = jnp.cumsum(delta_time * (-jnp.exp(log_rate))[None, :], axis=0)
    return (inputs, input_map, output_map, delta_time, cum_decay)

def mamba_out(inputs, input_map, output_map, delta_time, cum_decay, pair_mask, keep_first, skip_coef, gate, start_state):
    inside = pair_mask[:, :, None] > 0
    gaps = cum_decay[:, None, :] - cum_decay[None, :, :]
    decays = jnp.where(inside, jnp.exp(jnp.where(inside, gaps, 0.0)), 0.0)
    scores = jnp.dot(output_map, input_map.T, precision=highest)
    mixing = scores[:, :, None] * decays * delta_time[None, :, :]
    result = jnp.einsum('tsh,shp->thp', mixing, inputs, precision=highest)
    carried = jnp.einsum('tn,hpn->thp', output_map, start_state, precision=highest)
    result = result + carried * (jnp.exp(cum_decay) * keep_first[:, None])[:, :, None]
    result = result + skip_coef[None, :, None] * inputs
    return result.reshape(inputs.shape[0], -1) * jax.nn.silu(gate)

def reference(block_input, seg_ids, norm1_gain, zx_weight, dt_weight, bc_weight, conv_x_weight, conv_x_bias, conv_bc_weight, conv_bc_bias, dt_bias, a_log, d_skip, gnorm_gain, out_weight, q_weight, kv_weight, o_weight, norm2_gain, gu_weight, down_weight, d_out):
    conv_weight_all = jnp.concatenate([conv_x_weight, conv_bc_weight.astype(jnp.float32)], axis=1)
    conv_bias_all = jnp.concatenate([conv_x_bias, conv_bc_bias.astype(jnp.float32)])
    cos_table, sin_table = rope_tables(jnp.arange(LEN).astype(jnp.float32), ADIM)
    rows_all = jnp.arange(LEN)
    lower_mask = rows_all[:, None] >= rows_all[None, :]
    group_size = QH // KVH
    score_scale = ADIM ** (-0.5)
    zero_state = jnp.zeros((HEADS, HDIM, NST), jnp.float32)
    keep_none = jnp.zeros((LEN,), jnp.float32)
    gain_one = norm1_gain.astype(jnp.float32)
    gain_two = norm2_gain.astype(jnp.float32)
    weights_all = (norm1_gain, zx_weight, dt_weight, bc_weight, conv_x_weight, conv_x_bias, conv_bc_weight, conv_bc_bias, dt_bias, a_log, d_skip, gnorm_gain, out_weight, q_weight, kv_weight, o_weight, norm2_gain, gu_weight, down_weight)
    init_totals = tuple((jnp.zeros(weight.shape, jnp.float32) for weight in weights_all))

    def one_sequence(totals, row_in):
        x_row, seg_row, dout_row = row_in
        seg_ext = jnp.concatenate([jnp.full((KCONV - 1,), -1, jnp.int32), seg_row.astype(jnp.int32)])
        conv_keep = jnp.stack([seg_ext[offset:offset + LEN] == seg_row for offset in range(KCONV)]).astype(jnp.float32)
        same_doc = (seg_row[:, None] == seg_row[None, :]) & lower_mask
        pair_mask = same_doc.astype(jnp.float32)
        x_float = x_row.astype(jnp.float32)
        factor_one = rms_factor(x_float)
        normed_one = x_float * factor_one
        xn_bf = (normed_one * gain_one).astype(jnp.bfloat16)
        gate_bf = jnp.dot(xn_bf, zx_weight[0], preferred_element_type=jnp.float32).astype(jnp.bfloat16)
        xpre_bf = jnp.dot(xn_bf, zx_weight[1], preferred_element_type=jnp.float32).astype(jnp.bfloat16)
        dt_bf = jnp.dot(xn_bf, dt_weight, preferred_element_type=jnp.float32).astype(jnp.bfloat16)
        bc_bf = jnp.dot(xn_bf, bc_weight, preferred_element_type=jnp.float32).astype(jnp.bfloat16)
        pre_own = lax.optimization_barrier(jnp.concatenate([xpre_bf, bc_bf], axis=1)).astype(jnp.float32)
        pre_ext = jnp.concatenate([jnp.zeros((KCONV - 1, DI + 2 * NST), jnp.float32), pre_own], axis=0)
        gate_float = lax.optimization_barrier(gate_bf).astype(jnp.float32)
        dt_float = lax.optimization_barrier(dt_bf).astype(jnp.float32)

        def mamba_seq(pre_in, gate_in, dt_in, conv_weight, conv_bias, bias_dt, log_rate, skip_coef):
            sectioned = mamba_section(pre_in, dt_in, conv_weight, conv_bias, bias_dt, log_rate, conv_keep, DI)
            return mamba_out(sectioned[0], sectioned[1], sectioned[2], sectioned[3], sectioned[4], pair_mask, keep_none, skip_coef, gate_in, zero_state)
        mamba_flat, pull_back = jax.vjp(mamba_seq, pre_ext, gate_float, dt_float, conv_weight_all, conv_bias_all, dt_bias, a_log, d_skip)
        square_sum = lax.optimization_barrier(jnp.sum(mamba_flat * mamba_flat, axis=-1))
        gnorm_factor = lax.rsqrt(square_sum / DI + eps_norm)
        gained_bf = (mamba_flat * gnorm_gain[None, :]).astype(jnp.bfloat16)
        sm_full = jnp.dot(gained_bf, out_weight, preferred_element_type=jnp.float32)
        queries = jnp.dot(xn_bf, q_weight, preferred_element_type=jnp.float32).reshape(LEN, QH, ADIM)
        keyval = jnp.dot(xn_bf, kv_weight, preferred_element_type=jnp.float32).reshape(LEN, KVH, 2 * ADIM)
        queries_bf = rotate(queries, cos_table, sin_table).astype(jnp.bfloat16)
        keys_bf = rotate(keyval[..., :ADIM], cos_table, sin_table).astype(jnp.bfloat16)
        values_bf = keyval[..., ADIM:].astype(jnp.bfloat16)
        keys_rep = jnp.repeat(keys_bf, group_size, axis=1).astype(jnp.float32)
        values_rep = jnp.repeat(values_bf, group_size, axis=1).astype(jnp.float32)
        scores = jnp.einsum('qha,kha->hqk', queries_bf.astype(jnp.float32), keys_rep) * score_scale
        scores = jnp.where(same_doc[None], scores, -jnp.inf)
        row_max = lax.optimization_barrier(jnp.max(scores, axis=-1, keepdims=True))
        log_total = row_max + jnp.log(lax.optimization_barrier(jnp.sum(jnp.exp(scores - row_max), axis=-1, keepdims=True)))
        attn_probs = jnp.exp(scores - log_total)
        probs_bf = attn_probs.astype(jnp.bfloat16)
        attn_bf = jnp.einsum('hqk,kha->qha', probs_bf.astype(jnp.float32), values_rep).astype(jnp.bfloat16)
        attn_flat = attn_bf.reshape(LEN, QH * ADIM)
        sa_full = jnp.dot(attn_flat, o_weight, preferred_element_type=jnp.float32)
        hidden = x_float + gnorm_factor[:, None] * sm_full + sa_full
        factor_two = rms_factor(hidden)
        normed_two = hidden * factor_two
        hn_bf = (normed_two * gain_two).astype(jnp.bfloat16)
        gate_ff = jnp.dot(hn_bf, gu_weight[0], preferred_element_type=jnp.float32)
        up_ff = jnp.dot(hn_bf, gu_weight[1], preferred_element_type=jnp.float32)
        act_bf = (jax.nn.silu(gate_ff) * up_ff).astype(jnp.bfloat16)
        ffn_full = jnp.dot(act_bf, down_weight, preferred_element_type=jnp.float32)
        out_row = (hidden + ffn_full).astype(jnp.bfloat16)
        d_act = inner_cols(dout_row, down_weight)
        gate_sig = jax.nn.sigmoid(gate_ff)
        d_gate_ff = (d_act * up_ff * gate_sig * (1.0 + gate_ff * (1.0 - gate_sig))).astype(jnp.bfloat16)
        d_up_ff = (d_act * gate_ff * gate_sig).astype(jnp.bfloat16)
        grad_down = inner_rows(act_bf, dout_row)
        grad_gateup = jnp.stack([inner_rows(hn_bf, d_gate_ff), inner_rows(hn_bf, d_up_ff)])
        d_hn = inner_cols(d_gate_ff, gu_weight[0]) + inner_cols(d_up_ff, gu_weight[1])
        grad_gain_two = lax.optimization_barrier(jnp.sum(d_hn * normed_two, axis=0))
        d_hidden = dout_row.astype(jnp.float32) + rms_back(d_hn * gain_two, normed_two, factor_two)
        d_sm_bf = (gnorm_factor[:, None] * d_hidden).astype(jnp.bfloat16)
        dh_bf = d_hidden.astype(jnp.bfloat16)
        grad_mix_out = inner_rows(gained_bf, d_sm_bf)
        d_gained = inner_cols(d_sm_bf, out_weight)
        d_factor = lax.optimization_barrier(jnp.sum(d_hidden * sm_full, axis=-1))
        grad_gnorm = lax.optimization_barrier(jnp.sum(d_gained * mamba_flat, axis=0))
        d_mix = d_gained * gnorm_gain[None, :] - (d_factor * gnorm_factor ** 3 / DI)[:, None] * mamba_flat
        d_pre_ext, d_gate, d_dt, d_conv_weight, d_conv_bias, grad_dtb, grad_alog, grad_skip = pull_back(d_mix)
        d_pre = d_pre_ext[KCONV - 1:]
        d_gate_bf = d_gate.astype(jnp.bfloat16)
        d_xpre_bf = d_pre[:, :DI].astype(jnp.bfloat16)
        d_bc_bf = d_pre[:, DI:].astype(jnp.bfloat16)
        d_dt_bf = d_dt.astype(jnp.bfloat16)
        grad_attn_out = inner_rows(attn_flat, dh_bf)
        d_attn_bf = inner_cols(dh_bf, o_weight).astype(jnp.bfloat16).reshape(LEN, QH, ADIM)
        d_attn_float = d_attn_bf.astype(jnp.float32)
        delta_rows = jnp.einsum('qha,qha->hq', d_attn_float, attn_bf.astype(jnp.float32))
        d_values = jnp.einsum('hqk,qha->kha', probs_bf.astype(jnp.float32), d_attn_float).reshape(LEN, KVH, group_size, ADIM).sum(axis=2)
        d_probs = jnp.einsum('qha,kha->hqk', d_attn_float, values_rep)
        d_scores = (attn_probs * (d_probs - delta_rows[..., None])).astype(jnp.bfloat16).astype(jnp.float32)
        d_queries = jnp.einsum('hqk,kha->qha', d_scores, keys_rep) * score_scale
        d_keys = jnp.einsum('hqk,qha->kha', d_scores, queries_bf.astype(jnp.float32)).reshape(LEN, KVH, group_size, ADIM).sum(axis=2) * score_scale
        d_query_bf = rotate(d_queries, cos_table, -sin_table).astype(jnp.bfloat16).reshape(LEN, QH * ADIM)
        d_keys_back = rotate(d_keys, cos_table, -sin_table)
        d_kv_bf = jnp.concatenate([d_keys_back, d_values], axis=-1).astype(jnp.bfloat16).reshape(LEN, 2 * KVH * ADIM)
        d_xn = inner_cols(d_gate_bf, zx_weight[0]) + inner_cols(d_xpre_bf, zx_weight[1]) + inner_cols(d_dt_bf, dt_weight) + inner_cols(d_bc_bf, bc_weight) + inner_cols(d_query_bf, q_weight) + inner_cols(d_kv_bf, kv_weight)
        grad_gain_one = lax.optimization_barrier(jnp.sum(d_xn * normed_one, axis=0))
        dx_row = d_hidden + rms_back(d_xn * gain_one, normed_one, factor_one)
        terms = (grad_gain_one, jnp.stack([inner_rows(xn_bf, d_gate_bf), inner_rows(xn_bf, d_xpre_bf)]), inner_rows(xn_bf, d_dt_bf), inner_rows(xn_bf, d_bc_bf), d_conv_weight[:, :DI], d_conv_bias[:DI], d_conv_weight[:, DI:], d_conv_bias[DI:], grad_dtb, grad_alog, grad_skip, grad_gnorm, grad_mix_out, inner_rows(xn_bf, d_query_bf), inner_rows(xn_bf, d_kv_bf), grad_attn_out, grad_gain_two, grad_gateup, grad_down)
        new_totals = tuple((total + term for total, term in zip(totals, terms)))
        return (new_totals, (out_row, dx_row))
    totals, (block_out, input_grad) = lax.scan(one_sequence, init_totals, (block_input, seg_ids, d_out))
    return (block_out, input_grad, totals[0], totals[1], totals[2], totals[3], totals[4], totals[5], totals[6], totals[7], totals[8], totals[9], totals[10], totals[11], totals[12], totals[13], totals[14], totals[15], totals[16], totals[17], totals[18])
```

```python
import functools

import jax
import jax.numpy as jnp
from jax import lax
from jax.experimental import pallas as pl
from jax.experimental.pallas import tpu as pltpu
from jax.sharding import PartitionSpec as P

EPS = 1e-05
ROPE_BASE = 100000000000.0
HIGH = lax.Precision.HIGHEST
NEG = -1e30
F32 = jnp.float32
BF16 = jnp.bfloat16
GROUP = ("shard", "ctx")
LANES = 128
HALO = 8


def move(x, axis, pairs):
    return lax.ppermute(x, axis, pairs)


def xor_move(x, axis, size, mask):
    return move(x, axis, [(j, j ^ mask) for j in range(size)])


def gather_rows(x):
    shard, ctx = lax.axis_size("shard"), lax.axis_size("ctx")
    if shard != 4 or ctx != 2:
        return lax.all_gather(x, GROUP, axis=0, tiled=True)
    size = shard * ctx
    me = lax.axis_index(GROUP)
    core = (me // 2) % 2
    near_x = xor_move(x, GROUP, size, 1)
    near_y = xor_move(x, GROUP, size, 4)
    other = [xor_move(x, GROUP, size, 2)]
    pairs = [(j, j ^ 4 if (j // 2) % 2 == 0 else j ^ 1) for j in range(size)]
    far = move(jnp.where(core == 0, near_x, near_y), GROUP, pairs)
    other += [xor_move(piece, GROUP, size, 2) for piece in (near_x, near_y, far)]
    out = jnp.zeros((size,) + x.shape, x.dtype)
    for mask, piece in zip((0, 1, 4, 5, 2, 3, 6, 7), [x, near_x, near_y, far] + other):
        out = lax.dynamic_update_slice(out, piece[None], (jnp.bitwise_xor(me, mask), 0, 0))
    return out.reshape(size * x.shape[0], x.shape[1])


def scatter_rows(grad):
    shard, ctx = lax.axis_size("shard"), lax.axis_size("ctx")
    if shard != 4 or ctx != 2:
        return lax.psum_scatter(grad, GROUP, scatter_dimension=0, tiled=True)
    size = shard * ctx
    rows, width = grad.shape[0] // size, grad.shape[1]
    me = lax.axis_index(GROUP)
    y, core, c = me // 4, (me // 2) % 2, me % 2
    blocks = grad.reshape(2, 2, 2, rows, width)
    give = lax.dynamic_slice_in_dim(blocks, 1 - core, 1, axis=1).astype(BF16)
    keep = lax.dynamic_slice_in_dim(blocks, core, 1, axis=1)
    got = xor_move(give.reshape(4, rows, width), GROUP, size, 2)
    half = keep.reshape(4, rows, width) + got.astype(F32)
    pick = lambda yy, cc: lax.dynamic_index_in_dim(half, yy * 2 + cc, 0, False)
    total = pick(y, c)
    for mask, yy, cc in ((1, y, 1 - c), (4, 1 - y, c), (5, 1 - y, 1 - c)):
        total = total + xor_move(pick(yy, cc).astype(BF16), GROUP, size, mask).astype(F32)
    return total


def tp_all(x):
    n = lax.axis_size("tp")
    return [move(x, "tp", [(j, (j - k) % n) for j in range(n)]) for k in range(1, n)]


def tp_sum_small(x):
    total = x
    for other in tp_all(x):
        total = total + other
    return total


def tp_reduce(piece):
    n = lax.axis_size("tp")
    total = piece(0)
    for k in range(1, n):
        sent = move(piece(k).astype(BF16), "tp", [(j, (j + k) % n) for j in range(n)])
        total = total + sent.astype(F32)
    return total


def group_sum(x):
    size = lax.axis_size("shard") * lax.axis_size("ctx")
    mask = 1
    while mask < size:
        x = x + xor_move(x, GROUP, size, mask)
        mask *= 2
    return x


def call(body, outs, *args, scratch=()):
    spec = pl.BlockSpec(memory_space=pltpu.VMEM)
    return pl.pallas_call(
        body,
        out_shape=tuple(jax.ShapeDtypeStruct(s, d) for s, d in outs),
        in_specs=[spec] * len(args),
        out_specs=tuple([spec] * len(outs)),
        scratch_shapes=list(scratch),
        compiler_params=pltpu.CompilerParams(vmem_limit_bytes=60 * 1024 * 1024),
    )(*args)


def mm(a, b, dims=(1, 0), precision=HIGH):
    return lax.dot_general(
        a, b, (((dims[0],), (dims[1],)), ((), ())), precision=precision, preferred_element_type=F32
    )


def mb(a, b, dims=(1, 0)):
    return lax.dot_general(
        a, b, (((dims[0],), (dims[1],)), ((), ())), preferred_element_type=F32
    )


def iota(shape, axis):
    return lax.broadcasted_iota(jnp.int32, shape, axis)


def sigmoid(v):
    return 1.0 / (1.0 + jnp.exp(-v))


def expand(cols, width, hdim):
    per = LANES // hdim
    rows = cols.shape[0]
    parts = []
    for j in range(width // LANES):
        lane = iota((rows, LANES), 1)
        part = jnp.broadcast_to(cols[:, per * j : per * j + 1], (rows, LANES))
        for k in range(1, per):
            col = jnp.broadcast_to(cols[:, per * j + k : per * j + k + 1], (rows, LANES))
            part = jnp.where(lane >= k * hdim, col, part)
        parts.append(part)
    return jnp.concatenate(parts, axis=1)


def head_pick(width, hdim):
    return (iota((width, LANES), 0) // hdim == iota((width, LANES), 1)).astype(F32)


def swap_halves(x, half):
    lane = iota(x.shape, 1) % (2 * half)
    width = x.shape[1]
    return jnp.where(
        lane < half, pltpu.roll(x, width - half, axis=1), pltpu.roll(x, half, axis=1)
    )


def front_kernel(
    cfg, x_ref, gain_ref, w_ref, aux_ref, cw_ref, cb_ref, rate_ref, cq_ref, sq_ref, ck_ref, sk_ref,
    xn_ref, gate_ref, conv_ref, pre_ref, q_ref, send_ref, dt_ref, delta_ref, cum_ref,
):
    rows, inner, chan, heads, hdim, half = cfg
    x = x_ref[...].astype(F32)
    factor = lax.rsqrt(jnp.sum(x * x, axis=1, keepdims=True) / x.shape[1] + EPS)
    normed = x * factor * gain_ref[...]
    xn_ref[...] = normed[HALO:].astype(BF16)
    proj = mb(normed.astype(BF16), w_ref[...])
    gate_ref[...] = proj[HALO:, :inner].astype(BF16)
    pre_ref[...] = proj[:, inner : inner + chan].astype(BF16).astype(F32)
    taps = cw_ref.shape[0]
    conv = jnp.broadcast_to(cb_ref[...], (rows, chan))
    for o in range(taps):
        conv = conv + cw_ref[o : o + 1, :] * pre_ref[pl.ds(HALO - taps + 1 + o, rows), :] * aux_ref[
            :, o : o + 1
        ]
    conv_ref[...] = conv
    post = conv * sigmoid(conv)
    at = inner + chan
    q = proj[HALO:, at : at + LANES]
    q_ref[...] = (q * cq_ref[...] + swap_halves(q, half) * sq_ref[...]).astype(BF16)
    kv = proj[HALO:, at + LANES : at + 2 * LANES]
    send_ref[:rows, :] = (kv * ck_ref[...] + swap_halves(kv, half) * sk_ref[...]).astype(BF16)
    dt = proj[HALO:, at + 2 * LANES : at + 3 * LANES].astype(BF16).astype(F32) + rate_ref[0:1, :]
    live = iota((rows, LANES), 1) < heads
    dt = jnp.where(live, dt, 0.0)
    dt_ref[...] = dt
    delta = jnp.where(live, jnp.maximum(dt, 0.0) + jnp.log1p(jnp.exp(-jnp.abs(dt))), 0.0)
    delta_ref[...] = delta
    tri = (iota((rows, rows), 0) >= iota((rows, rows), 1)).astype(F32)
    cum = mm(tri, delta * rate_ref[1:2, :])
    cum_ref[...] = cum
    weight = jnp.exp(cum[rows - 1 :, :] - cum) * delta * aux_ref[:, 5:6]
    wx = expand(weight, inner, hdim) * post[:, :inner]
    nst = (chan - inner) // 2
    send_ref[rows:, :] = mm(wx, post[:, inner : inner + nst], (0, 0)).astype(BF16)


def mix_kernel(cfg, conv_ref, delta_ref, cum_ref, aux_ref, seg_ref, y_ref):
    rows, inner, chan, heads, hdim, half = cfg
    nst = (chan - inner) // 2
    conv = conv_ref[...]
    post = conv * sigmoid(conv)
    bmat, cmat = post[:, inner : inner + nst], post[:, inner + nst :]
    xd = expand(delta_ref[...], inner, hdim) * post[:, :inner]
    scores = mm(cmat, bmat, (1, 1))
    cum = cum_ref[...]
    cum_t = cum.T
    mask = (iota((rows, rows), 0) >= iota((rows, rows), 1)) & (aux_ref[:, 6:7] == seg_ref[0:1, :])
    per = LANES // hdim
    lane = iota((rows, LANES), 1) // hdim
    for j in range(inner // LANES):
        pair = xd[:, j * LANES : (j + 1) * LANES]
        total = jnp.zeros((rows, LANES), F32)
        for k in range(per):
            h = per * j + k
            gap = jnp.where(mask, cum[:, h : h + 1] - cum_t[h : h + 1, :], NEG)
            total = total + mm(scores * jnp.exp(gap), jnp.where(lane == k, pair, 0.0))
        y_ref[:, j * LANES : (j + 1) * LANES] = total


def finish_kernel(
    cfg, ylocal_ref, conv_ref, cum_ref, aux_ref, h0_ref, gate_ref, vec_ref, y_ref, gained_ref, sq_ref
):
    rows, inner, chan, heads, hdim, half = cfg
    nst = (chan - inner) // 2
    conv = conv_ref[...]
    post = conv * sigmoid(conv)
    carried = mm(post[:, inner + nst :], h0_ref[...].astype(F32), (1, 1))
    ek = jnp.exp(cum_ref[...]) * aux_ref[:, 4:5]
    y = ylocal_ref[...] + carried * expand(ek, inner, hdim) + vec_ref[0:1, :] * post[:, :inner]
    y_ref[...] = y
    gate = gate_ref[...].astype(F32)
    v = y * (gate * sigmoid(gate))
    gained_ref[...] = (v * vec_ref[1:2, :]).astype(BF16)
    sq_ref[...] = mm(jnp.ones((8, inner), F32), v * v, (1, 1))


def lane_half(x, k, width):
    lane = iota(x.shape, 1)
    keep = (lane >= k * width) & (lane < (k + 1) * width)
    return jnp.where(keep, x, jnp.zeros_like(x))


def attn_parts(adim, scale, q, kv, aux_ref, kseg_ref, rows, keys):
    kvr = pltpu.roll(kv.astype(F32), adim, axis=1).astype(BF16)
    place = iota((rows, keys), 1) - (keys - rows)
    mask = (place <= iota((rows, keys), 0)) & (aux_ref[:, 6:7] == kseg_ref[0:1, :])
    out = []
    for h in range(LANES // adim):
        key = kv if h == 0 else kvr
        s = mb(lane_half(q, h, adim), key, (1, 1)) * scale
        out.append(jnp.where(mask, s, NEG))
    return out, kvr


def attn_kernel(cfg, adim, q_ref, kv_ref, aux_ref, kseg_ref, attn_ref, lse_ref):
    rows = cfg[0]
    keys = kv_ref.shape[0]
    kv = kv_ref[...]
    scores, kvr = attn_parts(adim, adim**-0.5, q_ref[...], kv, aux_ref, kseg_ref, rows, keys)
    lane = iota((rows, LANES), 1)
    total = jnp.zeros((rows, LANES), F32)
    lses = jnp.zeros((rows, LANES), F32)
    for h, s in enumerate(scores):
        top = jnp.max(s, axis=1, keepdims=True)
        lse = top + jnp.log(jnp.sum(jnp.exp(s - top), axis=1, keepdims=True))
        probs = jnp.exp(s - lse).astype(BF16)
        value = lane_half(kvr if h == 0 else kv, h, adim)
        total = total + mb(probs, value)
        lses = jnp.where(lane == h, lse, lses)
    attn_ref[...] = total.astype(BF16)
    lse_ref[...] = lses


def attn_back_kernel(
    cfg, adim, q_ref, kv_ref, aux_ref, kseg_ref, attn_ref, lse_ref, da_ref, cq_ref, sq_ref, ck_ref, sk_ref,
    dq_ref, dkv_ref,
):
    rows, half = cfg[0], cfg[5]
    keys = kv_ref.shape[0]
    kv = kv_ref[...]
    q = q_ref[...]
    scale = adim**-0.5
    scores, kvr = attn_parts(adim, scale, q, kv, aux_ref, kseg_ref, rows, keys)
    da = da_ref[...]
    qr = pltpu.roll(q.astype(F32), adim, axis=1).astype(BF16)
    dar = pltpu.roll(da.astype(F32), adim, axis=1).astype(BF16)
    prod = da.astype(F32) * attn_ref[...].astype(F32)
    dq = jnp.zeros((rows, LANES), F32)
    dkey = jnp.zeros((keys, LANES), F32)
    dval = jnp.zeros((keys, LANES), F32)
    for h, s in enumerate(scores):
        probs = jnp.exp(s - lse_ref[:, h : h + 1])
        own = lane_half(da, h, adim)
        dp = mb(own, kvr if h == 0 else kv, (1, 1))
        dd = jnp.sum(lane_half(prod, h, adim), axis=1, keepdims=True)
        ds = (probs * (dp - dd)).astype(BF16)
        dq = dq + mb(ds, lane_half(kv if h == 0 else kvr, h, adim))
        dkey = dkey + mb(ds, lane_half(q if h == 0 else qr, 0, adim), (0, 0))
        dval = dval + mb(probs.astype(BF16), lane_half(dar if h == 0 else da, 1, adim), (0, 0))
    dq = dq * scale
    dq_ref[...] = (dq * cq_ref[...] - swap_halves(dq, half) * sq_ref[...]).astype(BF16)
    dkv_ref[...] = dkey * scale + dval


def back_gate_kernel(
    cfg, dg_ref, s_ref, y_ref, gate_ref, conv_ref, cum_ref, aux_ref, h0_ref, vec_ref,
    dy_ref, dgate_ref, dh0_ref, dc_ref, sums_ref,
):
    rows, inner, chan, heads, hdim, half = cfg
    nst = (chan - inner) // 2
    gate = gate_ref[...].astype(F32)
    sig = sigmoid(gate)
    act = gate * sig
    y = y_ref[...]
    v = y * act
    dgained = dg_ref[...]
    dv = dgained * vec_ref[1:2, :] - s_ref[:, 0:1] * v
    dy = dv * act
    dy_ref[...] = dy
    dgate_ref[...] = (dv * y * (sig * (1.0 + gate * (1.0 - sig)))).astype(BF16)
    conv = conv_ref[...]
    post = conv * sigmoid(conv)
    z = dy * expand(jnp.exp(cum_ref[...]) * aux_ref[:, 4:5], inner, hdim)
    dh0_ref[...] = mm(z, post[:, inner + nst :], (0, 0)).astype(BF16)
    dc_ref[...] = mm(z, h0_ref[...].astype(F32))
    sums_ref[0:1, :] = jnp.sum(dgained * v, axis=0, keepdims=True)
    sums_ref[1:2, :] = jnp.sum(dy * post[:, :inner], axis=0, keepdims=True)


def back_mix_kernel(
    cfg, conv_ref, delta_ref, cum_ref, aux_ref, seg_ref, dy_ref, dxs_ref, dd_ref, dbc_ref
):
    rows, inner, chan, heads, hdim, half = cfg
    nst = (chan - inner) // 2
    conv = conv_ref[...]
    post = conv * sigmoid(conv)
    bmat, cmat = post[:, inner : inner + nst], post[:, inner + nst :]
    delta = delta_ref[...]
    wide = expand(delta, inner, hdim)
    xs = post[:, :inner]
    xd = wide * xs
    dy = dy_ref[...]
    scores = mm(bmat, cmat, (1, 1))
    cum = cum_ref[...]
    cum_t = cum.T
    mask = (iota((rows, rows), 0) <= iota((rows, rows), 1)) & (aux_ref[:, 6:7] == seg_ref[0:1, :])
    per = LANES // hdim
    lane = iota((rows, LANES), 1) // hdim
    dscores = jnp.zeros((rows, rows), F32)
    parts = []
    for j in range(inner // LANES):
        dyp = dy[:, j * LANES : (j + 1) * LANES]
        xdp = xd[:, j * LANES : (j + 1) * LANES]
        total = jnp.zeros((rows, LANES), F32)
        for k in range(per):
            h = per * j + k
            dec = jnp.exp(jnp.where(mask, cum_t[h : h + 1, :] - cum[:, h : h + 1], NEG))
            dyh = jnp.where(lane == k, dyp, 0.0)
            total = total + mm(scores * dec, dyh)
            dscores = dscores + mm(xdp, dyh, (1, 1)) * dec
        parts.append(total)
    dxd = jnp.concatenate(parts, axis=1)
    dxs_ref[...] = wide * dxd
    dd_ref[...] = mm(xs * dxd, head_pick(inner, hdim))
    dbc_ref[:, :nst] = mm(dscores, cmat)
    dbc_ref[:, nst:] = mm(dscores, bmat, (0, 0))


def back_tail_kernel(
    cfg, conv_ref, pre_ref, delta_ref, cum_ref, dt_ref, aux_ref, rate_ref, cw_ref, vec_ref,
    dy_ref, y_ref, dxs_ref, dd_ref, dbc_ref, dc_ref, de_ref, h0_ref,
    dpre_ref, rim_ref, ddt_ref, wsum_ref, hsum_ref, buf_ref,
):
    rows, inner, chan, heads, hdim, half = cfg
    nst = (chan - inner) // 2
    conv = conv_ref[...]
    sig = sigmoid(conv)
    post = conv * sig
    xs, bmat = post[:, :inner], post[:, inner : inner + nst]
    delta, cum = delta_ref[...], cum_ref[...]
    rate = rate_ref[1:2, :]
    de, h0 = de_ref[...].astype(F32), h0_ref[...].astype(F32)
    dy = dy_ref[...]
    pick = head_pick(inner, hdim)
    tail = jnp.exp(cum[rows - 1 :, :] - cum) * aux_ref[:, 5:6]
    weight = tail * delta
    wide = expand(weight, inner, hdim)
    r = mm(bmat, de, (1, 1))
    skip = vec_ref[0:1, :]
    dxs = skip * dy + dxs_ref[...] + wide * r
    db = dbc_ref[:, :nst] + mm(wide * xs, de)
    dc = dbc_ref[:, nst:] + dc_ref[...]
    dweight = mm(xs * r, pick)
    moved = dweight * weight
    dd = dd_ref[...]
    dcum = mm(dy * (y_ref[...] - skip * xs), pick) - delta * dd - moved
    last = jnp.exp(cum[rows - 1 :, :]) * aux_ref[rows - 1 :, 4:5]
    dlast = mm(mm(jnp.ones((8, nst), F32), de * h0, (1, 1)), pick)[0:1, :]
    extra = jnp.sum(moved, axis=0, keepdims=True) + dlast * last
    dcum = dcum + jnp.where(iota((rows, LANES), 0) == rows - 1, extra, 0.0)
    tri = (iota((rows, rows), 0) <= iota((rows, rows), 1)).astype(F32)
    back = mm(tri, dcum)
    ddelta = dd + dweight * tail + back * rate
    ddt = ddelta * sigmoid(dt_ref[...])
    ddt = jnp.where(iota((rows, LANES), 1) < heads, ddt, 0.0)
    ddt_ref[...] = ddt.astype(BF16)
    hsum_ref[0:1, :] = jnp.sum(ddt, axis=0, keepdims=True)
    hsum_ref[1:2, :] = jnp.sum(back * delta, axis=0, keepdims=True) * rate
    dconv = jnp.concatenate([dxs, db, dc], axis=1) * (sig * (1.0 + conv * (1.0 - sig)))
    taps = cw_ref.shape[0]
    buf_ref[:HALO, :] = jnp.zeros((HALO, chan), F32)
    buf_ref[rows + HALO :, :] = jnp.zeros((HALO, chan), F32)
    dpre = jnp.zeros((rows, chan), F32)
    rim = jnp.zeros((HALO, chan), F32)
    for o in range(taps):
        kept = dconv * aux_ref[:, o : o + 1]
        wsum_ref[o : o + 1, :] = jnp.sum(
            kept * pre_ref[pl.ds(HALO - taps + 1 + o, rows), :], axis=0, keepdims=True
        )
        buf_ref[HALO : rows + HALO, :] = kept
        w = cw_ref[o : o + 1, :]
        dpre = dpre + w * buf_ref[pl.ds(HALO + taps - 1 - o, rows), :]
        rim = rim + w * buf_ref[pl.ds(taps - 1 - o, HALO), :]
    wsum_ref[taps : taps + 1, :] = jnp.sum(dconv, axis=0, keepdims=True)
    dpre_ref[...] = dpre
    rim_ref[...] = rim


def rope_tables(positions, adim, heads):
    half = adim // 2
    inverse = jnp.power(ROPE_BASE, -(jnp.arange(half).astype(F32) * 2.0 / adim))
    angles = positions[:, None] * inverse[None, :]
    cos, sin = jnp.cos(angles), jnp.sin(angles)
    cos1, sin1 = jnp.concatenate([cos, cos], 1), jnp.concatenate([-sin, sin], 1)
    return jnp.tile(cos1, (1, heads)), jnp.tile(sin1, (1, heads)), cos1, sin1


def lane_row(vec):
    return jnp.pad(vec.astype(F32), (0, LANES - vec.shape[0]))[None, :]


def cat(parts, axis=1):
    return jnp.concatenate(parts, axis=axis)


def local(
    block_input, seg_ids, norm1_gain, zx_weight, dt_weight, bc_weight, conv_x_weight, conv_x_bias,
    conv_bc_weight, conv_bc_bias, dt_bias, a_log, d_skip, gnorm_gain, out_weight, q_weight, kv_weight,
    o_weight, norm2_gain, gu_weight, down_weight, d_out,
):
    tp, ctx = lax.axis_size("tp"), lax.axis_size("ctx")
    t, c = lax.axis_index("tp"), lax.axis_index("ctx")
    size = lax.axis_size("shard") * ctx
    rows, width = block_input.shape[1], block_input.shape[2]
    shard_rows = width // size
    heads = dt_weight.shape[1]
    inner = zx_weight.shape[2]
    hdim = inner // heads
    taps = conv_x_weight.shape[0]
    nst = bc_weight.shape[1] // 2
    chan = inner + 2 * nst
    qwide = q_weight.shape[1]
    kvwide = kv_weight.shape[1]
    adim = kvwide // tp
    kvheads = kvwide // (2 * adim)
    per_kv = tp // kvheads
    ff = gu_weight.shape[2]
    part = rows // tp
    colw = 2 * nst // tp
    full_inner = inner * tp
    cfg = (rows, inner, chan, heads, hdim, adim // 2)

    own_kv = lax.dynamic_slice_in_dim(kv_weight, (t // per_kv) * 2 * adim, 2 * adim, axis=1)
    bias_col = jnp.zeros((shard_rows,), BF16).at[: conv_bc_bias.shape[0]].set(conv_bc_bias)
    misc = cat(
        [
            dt_weight,
            norm1_gain[:, None],
            norm2_gain[:, None],
            conv_bc_weight.T.reshape(shard_rows, 1),
            bias_col[:, None],
            jnp.zeros((shard_rows, LANES - heads - 4), BF16),
        ]
    )
    pack_a = cat([zx_weight[0], zx_weight[1], bc_weight, q_weight, own_kv, misc])
    wa = gather_rows(pack_a)
    pack_b = cat([gu_weight[0], gu_weight[1], out_weight.T, o_weight.T, down_weight.T])
    pack_b, _ = lax.optimization_barrier((pack_b, wa))
    wb = gather_rows(pack_b)

    x_own = block_input[0]
    halo = move(x_own[rows - HALO :], "ctx", [(j, j + 1) for j in range(ctx - 1)])
    x_ext = cat([halo, x_own], 0)

    start = c * rows
    pad_ids = cat([jnp.full((1, taps - 1), -1, jnp.int32), seg_ids])
    seg_ext = lax.dynamic_slice_in_dim(pad_ids, start, rows + taps - 1, axis=1)[0]
    seg_own = seg_ext[taps - 1 :]
    keeps = [(seg_ext[o : o + rows] == seg_own).astype(F32) for o in range(taps)]
    keep_first = (seg_own == seg_ext[taps - 2]).astype(F32)
    last_keep = (seg_own == seg_own[rows - 1]).astype(F32)
    segf = seg_own.astype(F32)
    zero = jnp.zeros_like(segf)
    aux = jnp.stack(keeps + [keep_first, last_keep, segf, zero], axis=1)
    seg_row = jnp.broadcast_to(segf[None, :], (8, rows))
    prev_seg = lax.dynamic_slice_in_dim(seg_ids[0], jnp.maximum(c - 1, 0) * rows, rows).astype(F32)
    prev_seg = jnp.where(c > 0, prev_seg, -1.0)
    kseg = jnp.broadcast_to(cat([prev_seg, segf], 0)[None, :], (8, 2 * rows))
    positions = (start + jnp.arange(rows)).astype(F32)
    cos_q, sin_q, cos_1, sin_1 = rope_tables(positions, adim, qwide // adim)
    cos_k = cat([cos_1, jnp.ones((rows, adim), F32)])
    sin_k = cat([sin_1, jnp.zeros((rows, adim), F32)])
    rate = cat([lane_row(dt_bias), lane_row(-jnp.exp(a_log))] + [jnp.zeros((6, LANES), F32)], 0)

    at = inner + chan + qwide + 2 * adim + heads
    small = wa[:, at : at + 4].T
    gain1, gain2 = small[0:1].astype(F32), small[1:2].astype(F32)
    cw_bc = small[2].reshape(2 * nst, taps).T.astype(F32)
    cb_bc = small[3].reshape(size, shard_rows)[:, : 2 * nst // size].reshape(1, 2 * nst).astype(F32)
    cw = cat([conv_x_weight, cw_bc])
    cb = cat([conv_x_bias[None, :], cb_bc])
    vec = cat([jnp.repeat(d_skip, hdim)[None, :], gnorm_gain[None, :]], 0)

    xn, gate, conv, pre, q, send, dt, delta, cum = call(
        functools.partial(front_kernel, cfg),
        [
            ((rows, width), BF16),
            ((rows, inner), BF16),
            ((rows, chan), F32),
            ((rows + HALO, chan), F32),
            ((rows, LANES), BF16),
            ((rows + inner, LANES), BF16),
            ((rows, LANES), F32),
            ((rows, LANES), F32),
            ((rows, LANES), F32),
        ],
        x_ext, gain1, wa, aux, cw, cb, rate, cos_q, sin_q, cos_k, sin_k,
    )
    came = move(send, "ctx", [(j, j + 1) for j in range(ctx - 1)])
    (ylocal,) = call(
        functools.partial(mix_kernel, cfg), [((rows, inner), F32)], conv, delta, cum, aux, seg_row
    )
    h0 = came[rows:]
    kv_all = cat([came[:rows], send[:rows]], 0)
    y, gained, sq = call(
        functools.partial(finish_kernel, cfg),
        [((rows, inner), F32), ((rows, inner), BF16), ((8, rows), F32)],
        ylocal, conv, cum, aux, h0, gate, vec,
    )
    square = tp_sum_small(sq)[0]
    attn, lse = call(
        functools.partial(attn_kernel, cfg, adim),
        [((rows, LANES), BF16), ((rows, LANES), F32)],
        q, kv_all, aux, kseg,
    )
    rr = lax.rsqrt(square / full_inner + EPS)[:, None]
    w_gu = wb[:, : 2 * ff]
    w_out = wb[:, 2 * ff : 2 * ff + inner]
    w_o = wb[:, 2 * ff + inner : 2 * ff + inner + qwide]
    w_down = wb[:, 2 * ff + inner + qwide :]
    both = rr * mb(gained, w_out, (1, 1)) + mb(attn, w_o, (1, 1))
    both3 = both.reshape(tp, part, width)
    rank = lambda k: (t + k) % tp
    pick3 = lambda k: lax.dynamic_index_in_dim(both3, rank(k), 0, False)
    mixed = tp_reduce(pick3)

    mine = lambda a: lax.dynamic_slice_in_dim(a, t * part, part, axis=0)
    x_mine = mine(x_own).astype(F32)
    hidden = x_mine + mixed
    fac2 = lax.rsqrt(jnp.sum(hidden * hidden, axis=1, keepdims=True) / width + EPS)
    hhat = hidden * fac2
    hn_mine = (hhat * gain2).astype(BF16)
    hn = cat([hn_mine] + tp_all(hn_mine), 0)
    turned = lambda a, k: lax.dynamic_slice_in_dim(cat([a, a], 0), k * part, rows, axis=0)
    dout = turned(d_out[0], t)
    d_act = mb(dout, w_down)
    gu = mb(hn, w_gu)
    gff, uff = gu[:, :ff], gu[:, ff:]
    sig = jax.nn.sigmoid(gff)
    act = (gff * sig * uff).astype(BF16)
    dgff = (d_act * uff * sig * (1.0 + gff * (1.0 - sig))).astype(BF16)
    duff = (d_act * gff * sig).astype(BF16)
    dgu = cat([dgff, duff])
    dhn_part = mb(dgu, w_gu, (1, 1))
    slot = lambda a: (lambda k: a[k * part : (k + 1) * part])
    dhn = tp_reduce(slot(dhn_part))
    ffn_part = mb(act, w_down, (1, 1))
    grad_b1 = cat([mb(hn, dgu, (0, 0)), mb(dout, act, (0, 0))])

    sum_gain2 = jnp.sum(dhn * hhat, axis=0)
    e2 = dhn * gain2
    dhid = mine(d_out[0]).astype(F32) + fac2 * (
        e2 - hhat * (jnp.sum(e2 * hhat, axis=1, keepdims=True) / width)
    )
    dh_mine = dhid.astype(BF16)
    dh_rot = cat([dh_mine] + tp_all(dh_mine), 0)
    dh = turned(dh_rot, (tp - t) % tp)
    owned_b1 = scatter_rows(grad_b1)

    dsm = (rr * dh.astype(F32)).astype(BF16)
    dgained = mb(dsm, w_out)
    cross = jnp.sum(gained.astype(F32) * dgained, axis=1)
    cross = tp_sum_small(jnp.broadcast_to(cross[None, :], (8, rows)))[0]
    coef = (cross * jnp.square(rr[:, 0]) / full_inner)[:, None]
    d_attn = mb(dh, w_o).astype(BF16)
    dq, dkv_all = call(
        functools.partial(attn_back_kernel, cfg, adim),
        [((rows, LANES), BF16), ((2 * rows, LANES), F32)],
        q, kv_all, aux, kseg, attn, lse, d_attn, cos_q, sin_q, cos_k, sin_k,
    )
    dy, dgate, dh0, dc1, gsums = call(
        functools.partial(back_gate_kernel, cfg),
        [
            ((rows, inner), F32),
            ((rows, inner), BF16),
            ((inner, nst), BF16),
            ((rows, nst), F32),
            ((2, inner), F32),
        ],
        dgained, coef, y, gate, conv, cum, aux, h0, vec,
    )
    back_pairs = [(j + 1, j) for j in range(ctx - 1)]
    de = move(dh0, "ctx", back_pairs)
    dxs, ddel, dbc = call(
        functools.partial(back_mix_kernel, cfg),
        [((rows, inner), F32), ((rows, LANES), F32), ((rows, 2 * nst), F32)],
        conv, delta, cum, aux, seg_row, dy,
    )
    dpre, rim, ddt, wsum, hsum = call(
        functools.partial(back_tail_kernel, cfg),
        [
            ((rows, chan), F32),
            ((HALO, chan), F32),
            ((rows, LANES), BF16),
            ((taps + 1, chan), F32),
            ((2, LANES), F32),
        ],
        conv, pre, delta, cum, dt, aux, rate, cw, vec, dy, y, dxs, ddel, dbc, dc1, de, h0,
        scratch=[pltpu.VMEM((rows + 2 * HALO, chan), F32)],
    )
    block_rows = cat([dkv_all[:rows], rim.reshape(-1, LANES)], 0).astype(BF16)
    came_back = move(block_rows, "ctx", back_pairs).astype(F32)
    dkv = dkv_all[rows:] + came_back[:rows]
    rim_in = came_back[rows:].reshape(HALO, chan)
    dpre = dpre.at[rows - HALO :].add(rim_in)
    grad_b2 = cat([mb(dsm, gained, (0, 0)), mb(dh, attn, (0, 0))])

    dkv = dkv * cos_k - cat([dkv[:, adim // 2 : adim], dkv[:, : adim // 2], dkv[:, adim:]]) * sin_k
    dbc4 = dpre[:, inner:].reshape(rows, tp, colw)
    bc_piece = lambda r: lax.dynamic_index_in_dim(dbc4, r, 1, False)
    dkv4 = dkv.reshape(rows, per_kv, 2 * adim // per_kv)
    kv_piece = lambda r: lax.dynamic_index_in_dim(dkv4, r, 1, False)
    dbc_own = bc_piece(t)
    dkv_own = kv_piece(t % per_kv)
    for k in range(1, tp):
        peer = jnp.bitwise_xor(t, k)
        item = bc_piece(peer)
        if k < per_kv:
            item = cat([item, kv_piece(peer % per_kv)])
        item = xor_move(item.astype(BF16), "tp", tp, k).astype(F32)
        dbc_own = dbc_own + item[:, :colw]
        if k < per_kv:
            dkv_own = dkv_own + item[:, colw:]
    wcol = lax.dynamic_slice_in_dim(wa, 2 * inner + t * colw, colw, axis=1)
    kcol = lax.dynamic_slice_in_dim(
        wa, inner + chan + qwide + (t % per_kv) * (2 * adim // per_kv), 2 * adim // per_kv, axis=1
    )
    w_back = cat(
        [wa[:, : 2 * inner], wa[:, inner + chan : inner + chan + qwide], wa[:, at - heads :], wcol, kcol]
    )
    d_all = cat(
        [dgate, dpre[:, :inner].astype(BF16), dq, ddt, dbc_own.astype(BF16), dkv_own.astype(BF16)]
    )
    dxn_part = mb(d_all, w_back, (1, 1)).reshape(tp, part, width)
    dxn = tp_reduce(lambda k: lax.dynamic_index_in_dim(dxn_part, rank(k), 0, False))
    grad_a = mb(xn, d_all, (0, 0))
    owned_b2 = scatter_rows(grad_b2)
    owned_a = scatter_rows(grad_a)

    fac1 = lax.rsqrt(jnp.sum(x_mine * x_mine, axis=1, keepdims=True) / width + EPS)
    xhat = x_mine * fac1
    sum_gain1 = jnp.sum(dxn * xhat, axis=0)
    e1 = dxn * gain1
    ig_mine = dhid + fac1 * (e1 - xhat * (jnp.sum(e1 * xhat, axis=1, keepdims=True) / width))
    ffn = tp_reduce(slot(ffn_part))
    bo_mine = (hidden + ffn).astype(BF16)
    true_order = lambda a: turned(cat([a] + tp_all(a), 0), (tp - t) % tp)
    block_out = true_order(bo_mine)
    input_grad = true_order(ig_mine.astype(BF16)).astype(F32)

    wide_sums = cat(
        [sum_gain1.reshape(-1, LANES), sum_gain2.reshape(-1, LANES), wsum[:, inner:].reshape(-1, LANES)], 0
    )
    wide_sums = tp_sum_small(wide_sums)
    n_wide = wide_sums.shape[0]
    head_rows = cat([wsum[:, :inner].reshape(-1, LANES), gsums.reshape(-1, LANES), hsum], 0)
    sums = group_sum(cat([wide_sums, head_rows], 0))
    gain_rows = width // LANES
    mine8 = lambda a, n, axis: lax.dynamic_slice_in_dim(a, lax.axis_index(GROUP) * n, n, axis=axis)
    g_norm1 = mine8(sums[:gain_rows].reshape(width), shard_rows, 0)
    g_norm2 = mine8(sums[gain_rows : 2 * gain_rows].reshape(width), shard_rows, 0)
    conv_bc = sums[2 * gain_rows : n_wide].reshape(taps + 1, 2 * nst)
    conv_bc = mine8(conv_bc, 2 * nst // size, 1)
    rest = sums[n_wide:]
    n_conv = (taps + 1) * inner // LANES
    conv_x = rest[:n_conv].reshape(taps + 1, inner)
    gs = rest[n_conv : n_conv + 2 * inner // LANES].reshape(2, inner)
    hs = rest[n_conv + 2 * inner // LANES :]

    cut = [0, inner, 2 * inner, 2 * inner + qwide, 2 * inner + qwide + LANES]
    g_zx = jnp.stack([owned_a[:, : cut[1]], owned_a[:, cut[1] : cut[2]]])
    g_q = owned_a[:, cut[2] : cut[3]]
    g_dt = owned_a[:, cut[3] : cut[3] + heads]
    cols = owned_a[:, cut[4] :]
    turned_cols = cat([cols[None]] + [o[None] for o in tp_all(cols)], 0)
    order = lax.dynamic_slice_in_dim(cat([turned_cols, turned_cols], 0), (tp - t) % tp, tp, axis=0)
    g_bc = order[:, :, :colw].transpose(1, 0, 2).reshape(shard_rows, 2 * nst)
    g_kv = order[:, :, colw:].transpose(1, 0, 2).reshape(shard_rows, kvwide)
    return (
        block_out[None],
        input_grad[None],
        g_norm1,
        g_zx,
        g_dt,
        g_bc,
        conv_x[:taps],
        conv_x[taps],
        conv_bc[:taps],
        conv_bc[taps],
        hs[0, :heads],
        hs[1, :heads],
        gs[1].reshape(heads, hdim).sum(axis=1),
        gs[0],
        owned_b2[:, :inner].T,
        g_q,
        g_kv,
        owned_b2[:, inner:].T,
        g_norm2,
        jnp.stack([owned_b1[:, :ff], owned_b1[:, ff : 2 * ff]]),
        owned_b1[:, 2 * ff :].T,
    )


def solution(mesh):
    group = ("shard", "ctx")
    weight = P(None, group, "tp")
    ins = (
        P("shard", "ctx", None), P("shard", None), P(group), weight, P(group, "tp"), P(group, None),
        P(None, "tp"), P("tp"), P(None, group), P(group), P("tp"), P("tp"), P("tp"), P("tp"),
        P("tp", group), P(group, "tp"), P(group, None), P("tp", group), P(group), weight,
        P("tp", group), P("shard", "ctx", None),
    )
    outs = (P("shard", "ctx", None), P("shard", "ctx", None)) + ins[2:21]
    return jax.shard_map(local, mesh=mesh, in_specs=ins, out_specs=outs, check_vma=False)
```
